32 devices in a mesh: gx: 2 (over x), gy: 4 (over y, core), gz: 4 (over z).
Axes of the slice: x: 2, y: 2, z: 4, core: 2. Of those that a mesh axis runs over, the one named last changes fastest.
Arguments:
- conserved: float32 [5, 16, 32, 256], P(None, 'gz', 'gy', 'gx'), may hold values from -3 to 12, as said below
- metrics: float32 [9, 16, 32, 256], P(None, 'gz', 'gy', 'gx'), may hold values from -0.6 to 2, as said below
- inv_volume: float32 [16, 32, 256], P('gz', 'gy', 'gx'), may hold values from 0.5 to 2
- wake_donor: int32 [256], P('gx'), may hold values from -1 to 255, as said below
Outputs:
- section_state: float32 [5, 16, 32, 256], P(None, 'gz', 'gy', 'gx')
- time_rate: float32 [5, 16, 32, 256], P(None, 'gz', 'gy', 'gx')
The draws below stay inside these ranges and needn't reach their ends.
Inputs may be any that keep to these rules, and one draw needn't show every extreme that they name: `conserved`: each cell holds density rho of 0.5 to 2, pressure p of 0.5 to 2 and velocity components u of -1.5 to 1.5 as (rho, rho u, p / 0.4 + rho |u|^2 / 2). `metrics`: in each cell, row d (entries 3 d to 3 d + 2) has its entry 3 d + d between 0.5 and 2 and its other two entries at most 0.3 times that entry in magnitude. wake_donor[i] is either 256 - 1 - i or -1, and wake_donor[i] >= 0 exactly where wake_donor[255 - i] >= 0.
All inputs are finite; a program needn't handle non-finite values.
Results may differ from the reference program's by a relative error of at most 0.0001.
Values sent between devices are 32-bit elements; how exact they have to be, the bound alone decides.
A program may use at most 64 MiB of HBM per device.

```python
import math
import jax
import jax.numpy as jnp
from jax import lax

CY = 8
CZ = 4
NX = 256
NY = 32
NZ = 16


def draw_conserved(key, part):
    subkeys = jax.random.split(key, 3)
    grid_shape = (NZ, NY, NX)
    density = jnp.exp(jax.random.uniform(subkeys[0], grid_shape, jnp.float32, -0.6931, 0.6931))
    pressure = jnp.exp(jax.random.uniform(subkeys[1], grid_shape, jnp.float32, -0.6931, 0.6931))
    velocity = jnp.clip(0.5 * jax.random.normal(subkeys[2], (3,) + grid_shape, jnp.float32), -1.5, 1.5)
    energy = pressure / 0.4 + 0.5 * density * jnp.sum(velocity * velocity, axis=0)
    return jnp.concatenate([density[None], density[None] * velocity, energy[None]], axis=0).astype(jnp.float32)


def draw_metrics(key, part):
    subkeys = jax.random.split(key, 2)
    grid_shape = (NZ, NY, NX)
    diagonal = jnp.exp(jax.random.uniform(subkeys[0], (3,) + grid_shape, jnp.float32, -0.6931, 0.6931))
    ratios = jax.random.uniform(subkeys[1], (3, 3) + grid_shape, jnp.float32, -0.3, 0.3)
    entries = []
    for direction in range(3):
        for component in range(3):
            if component == direction:
                entries.append(diagonal[direction])
            else:
                entries.append(ratios[direction, component] * diagonal[direction])
    return jnp.stack(entries).astype(jnp.float32)


def draw_wake_donor(key, part):
    own_key = jax.random.fold_in(key, 4177)
    half_flags = jax.random.randint(own_key, (NX // 2,), 0, 2).astype(jnp.int32)
    flags = jnp.concatenate([half_flags, half_flags[::-1]], axis=0)
    column = jnp.arange(NX, dtype=jnp.int32)
    return jnp.where(flags > 0, NX - 1 - column, -1).astype(jnp.int32)


def steps_of(rng, shape, shards, low, top_value):
    def one(dim, parts):
        steps = jax.random.uniform(jax.random.fold_in(jax.random.fold_in(rng, 6), dim), (parts,), jnp.float32, low / len(shards), top_value / len(shards))
        return jnp.repeat(jnp.exp(steps), shape[dim] // parts).reshape((-1,) + (1,) * (len(shape) - dim - 1))

    gain = one(*shards[0])
    for cut in shards[1:]:
        gain = gain * one(*cut)
    return gain


def setup_inputs(seed: int = 0) -> dict:
    streams_of = jax.random.split(jax.random.key(seed), 5)
    return {
        "conserved": draw_conserved(jax.random.fold_in(streams_of[4], 71), 0),
        "metrics": draw_metrics(jax.random.fold_in(streams_of[4], 71), 0),
        "inv_volume": jnp.clip(jnp.exp(math.log(2.0) - 1.3862944 * jax.random.uniform(streams_of[2], (NZ, NY, NX), jnp.float32) ** steps_of(streams_of[2], (NZ, NY, NX), ((0, 4), (1, 4), (2, 2)), -0.2, 0.2)), 0.5, 2.0),
        "wake_donor": draw_wake_donor(jax.random.fold_in(streams_of[4], 71), 0),
    }


GAMMA = 1.4
WENO_EPS = 1e-06
STEP_SIZE = 0.08

def slab_of(values, start, amount, axis):
    return lax.slice_in_dim(values, start, start + amount, axis=values.ndim + axis)

def cross_of(first, second):
    return [first[1] * second[2] - first[2] * second[1], first[2] * second[0] - first[0] * second[2], first[0] * second[1] - first[1] * second[0]]

def inner_of(first, second):
    return first[0] * second[0] + first[1] * second[1] + first[2] * second[2]

def cell_terms(fields, metric_row):
    density = fields[0]
    velocity = fields[1:4] / density
    kinetic = 0.5 * lax.optimization_barrier(jnp.sum(fields[1:4] * velocity, axis=0))
    pressure = (GAMMA - 1.0) * (fields[4] - kinetic)
    contra = lax.optimization_barrier(jnp.sum(metric_row * velocity, axis=0))
    fluxes = jnp.stack([fields[0] * contra, fields[1] * contra + metric_row[0] * pressure, fields[2] * contra + metric_row[1] * pressure, fields[3] * contra + metric_row[2] * pressure, (fields[4] + pressure) * contra])
    sound_speed = jnp.sqrt(GAMMA * pressure / density)
    speeds = jnp.abs(contra) + sound_speed * jnp.sqrt(lax.optimization_barrier(jnp.sum(metric_row * metric_row, axis=0)))
    primitive = jnp.concatenate([density[None], velocity, pressure[None]], axis=0)
    return (primitive, fluxes, speeds)

def eigen_pair(state, metric_row, pick):
    density = state[0]
    velocity = [state[1], state[2], state[3]]
    pressure = state[4]
    row_size = jnp.sqrt(metric_row[0] ** 2 + metric_row[1] ** 2 + metric_row[2] ** 2)
    normal = [metric_row[member] / row_size for member in range(3)]
    axis_unit = [1.0 if member == pick else 0.0 for member in range(3)]
    raw_cross = cross_of(normal, axis_unit)
    raw_size = jnp.sqrt(raw_cross[0] ** 2 + raw_cross[1] ** 2 + raw_cross[2] ** 2)
    tangent = [raw_cross[member] / raw_size for member in range(3)]
    binormal = cross_of(normal, tangent)
    sound_speed = jnp.sqrt(GAMMA * pressure / density)
    inverse = 1.0 / sound_speed
    kinetic = 0.5 * inner_of(velocity, velocity)
    enthalpy = GAMMA / (GAMMA - 1.0) * pressure / density + kinetic
    normal_speed = inner_of(normal, velocity)
    tangent_speed = inner_of(tangent, velocity)
    binormal_speed = inner_of(binormal, velocity)
    factor = (GAMMA - 1.0) * inverse * inverse
    scaled = factor * kinetic
    left_rows = [[0.5 * (scaled + normal_speed * inverse)] + [0.5 * (-factor * velocity[member] - normal[member] * inverse) for member in range(3)] + [0.5 * factor], [1.0 - scaled] + [factor * velocity[member] for member in range(3)] + [-factor], [-tangent_speed] + tangent + [0.0], [-binormal_speed] + binormal + [0.0], [0.5 * (scaled - normal_speed * inverse)] + [0.5 * (-factor * velocity[member] + normal[member] * inverse) for member in range(3)] + [0.5 * factor]]
    right_columns = [[1.0] + [velocity[member] - sound_speed * normal[member] for member in range(3)] + [enthalpy - sound_speed * normal_speed], [1.0] + velocity + [kinetic], [0.0] + tangent + [tangent_speed], [0.0] + binormal + [binormal_speed], [1.0] + [velocity[member] + sound_speed * normal[member] for member in range(3)] + [enthalpy + sound_speed * normal_speed]]
    return (left_rows, right_columns)

def project_left(matrix, vector):
    return jnp.stack([sum((matrix[member][second] * vector[second] for second in range(5))) for member in range(5)])

def apply_right(matrix, vector):
    return jnp.stack([sum((matrix[second][member] * vector[second] for second in range(5))) for member in range(5)])

def weno_side(stencil):
    far_left, near_left, center, near_right, far_right = stencil
    guess_zero = (2.0 * far_left - 7.0 * near_left + 11.0 * center) / 6.0
    guess_one = (-near_left + 5.0 * center + 2.0 * near_right) / 6.0
    guess_two = (2.0 * center + 5.0 * near_right - far_right) / 6.0
    smooth_zero = 13.0 / 12.0 * (far_left - 2.0 * near_left + center) ** 2 + 0.25 * (far_left - 4.0 * near_left + 3.0 * center) ** 2
    smooth_one = 13.0 / 12.0 * (near_left - 2.0 * center + near_right) ** 2 + 0.25 * (near_left - near_right) ** 2
    smooth_two = 13.0 / 12.0 * (center - 2.0 * near_right + far_right) ** 2 + 0.25 * (3.0 * center - 4.0 * near_right + far_right) ** 2
    weight_zero = 0.1 / (WENO_EPS + smooth_zero) ** 2
    weight_one = 0.6 / (WENO_EPS + smooth_one) ** 2
    weight_two = 0.3 / (WENO_EPS + smooth_two) ** 2
    return (weight_zero * guess_zero + weight_one * guess_one + weight_two * guess_two) / (weight_zero + weight_one + weight_two)

def interface_flux(fields, metric_row, axis, pick):
    primitive, fluxes, speeds = cell_terms(fields, metric_row)
    faces_count = fields.shape[fields.ndim + axis] - 5
    mean_state = 0.5 * (slab_of(primitive, 2, faces_count, axis) + slab_of(primitive, 3, faces_count, axis))
    mean_row = 0.5 * (slab_of(metric_row, 2, faces_count, axis) + slab_of(metric_row, 3, faces_count, axis))
    left_rows, right_columns = eigen_pair(mean_state, mean_row, pick)
    max_speed = slab_of(speeds, 0, faces_count, axis)
    for offset in range(1, 6):
        max_speed = jnp.maximum(max_speed, slab_of(speeds, offset, faces_count, axis))
    upwind = []
    downwind = []
    for offset in range(6):
        state_chars = project_left(left_rows, slab_of(fields, offset, faces_count, axis))
        flux_chars = project_left(left_rows, slab_of(fluxes, offset, faces_count, axis))
        upwind.append(0.5 * (flux_chars + max_speed * state_chars))
        downwind.append(0.5 * (flux_chars - max_speed * state_chars))
    combined = weno_side(upwind[0:5]) + weno_side(downwind[5:0:-1])
    return apply_right(right_columns, combined)

def divergence(fields, metric_row, axis, pick):
    face_flux = interface_flux(fields, metric_row, axis, pick)
    cells_count = face_flux.shape[face_flux.ndim + axis] - 1
    return slab_of(face_flux, 1, cells_count, axis) - slab_of(face_flux, 0, cells_count, axis)

def blocked(fields, metric_row, axis, pick, block_dim, block):
    pieces = fields.shape[block_dim] // block

    def one_block(start):
        flow_part = lax.dynamic_slice_in_dim(fields, start, block, block_dim)
        row_part = lax.dynamic_slice_in_dim(metric_row, start, block, block_dim)
        return divergence(flow_part, row_part, axis, pick)
    starts = jnp.arange(pieces, dtype=jnp.int32) * block
    stacked = lax.map(one_block, starts)
    moved = jnp.moveaxis(stacked, 0, block_dim)
    dims = list(moved.shape)
    merged = dims[:block_dim] + [pieces * block] + dims[block_dim + 2:]
    return moved.reshape(merged)

def reference(conserved, metrics, inv_volume, wake_donor):
    edge_pad = ((0, 0), (0, 0), (0, 0), (3, 3))
    stream_flow = jnp.pad(conserved, edge_pad, mode='edge')
    stream_row = jnp.pad(metrics[0:3], edge_pad, mode='edge')
    momentum_sign = jnp.array([1.0, -1.0, -1.0, -1.0, 1.0], dtype=jnp.float32)[:, None, None, None]
    below_wall = conserved[:, :, 2::-1, :]
    below_row = metrics[3:6, :, 2::-1, :]
    is_wake = wake_donor >= 0
    source_column = jnp.where(is_wake, wake_donor, 0).astype(jnp.int32)
    low_flow = jnp.where(is_wake, jnp.take(below_wall, source_column, axis=3), below_wall * momentum_sign)
    low_row = jnp.where(is_wake, jnp.take(below_row, source_column, axis=3), below_row)
    normal_flow = jnp.concatenate([low_flow, conserved, jnp.repeat(conserved[:, :, -1:, :], 3, axis=2)], axis=2)
    normal_row = jnp.concatenate([low_row, metrics[3:6], jnp.repeat(metrics[3:6, :, -1:, :], 3, axis=2)], axis=2)
    span_flow = jnp.concatenate([conserved[:, -3:], conserved, conserved[:, :3]], axis=1)
    span_metric = metrics[6:9]
    span_row = jnp.concatenate([span_metric[:, -3:], span_metric, span_metric[:, :3]], axis=1)
    summed = blocked(stream_flow, stream_row, -1, 1, 1, CZ)
    summed = summed + blocked(normal_flow, normal_row, -2, 2, 1, CZ)
    summed = summed + blocked(span_flow, span_row, -3, 0, 2, CY)
    time_rate = -inv_volume[None] * summed
    return (conserved + STEP_SIZE * time_rate, time_rate)
```

```python
import jax
import jax.numpy as jnp
from jax import lax
from jax.sharding import PartitionSpec as P

GAMMA = 1.4
WENO_EPS = 1e-06
STEP_SIZE = 0.08


def padded(block, sides, width, periodic):
    for axis, dim in sides:
        count = lax.axis_size(axis)
        forward = [(i, i + 1) for i in range(count - 1)]
        if periodic:
            forward.append((count - 1, 0))
        backward = [(target, source) for source, target in forward]
        low = lax.ppermute(
            lax.slice_in_dim(block, block.shape[dim] - width, None, axis=dim), axis, forward
        )
        high = lax.ppermute(lax.slice_in_dim(block, 0, width, axis=dim), axis, backward)
        block = jnp.concatenate([low, block, high], axis=dim)
    return block


def slab_of(values, start, amount, axis):
    return lax.slice_in_dim(values, start, start + amount, axis=values.ndim + axis)


def cross_of(first, second):
    return [
        first[1] * second[2] - first[2] * second[1],
        first[2] * second[0] - first[0] * second[2],
        first[0] * second[1] - first[1] * second[0],
    ]


def inner_of(first, second):
    return first[0] * second[0] + first[1] * second[1] + first[2] * second[2]


def cell_terms(fields, metric_row):
    density = fields[0]
    velocity = fields[1:4] / density
    kinetic = 0.5 * jnp.sum(fields[1:4] * velocity, axis=0)
    pressure = (GAMMA - 1.0) * (fields[4] - kinetic)
    contra = jnp.sum(metric_row * velocity, axis=0)
    fluxes = jnp.stack(
        [
            fields[0] * contra,
            fields[1] * contra + metric_row[0] * pressure,
            fields[2] * contra + metric_row[1] * pressure,
            fields[3] * contra + metric_row[2] * pressure,
            (fields[4] + pressure) * contra,
        ]
    )
    sound_speed = jnp.sqrt(GAMMA * pressure / density)
    speeds = jnp.abs(contra) + sound_speed * jnp.sqrt(jnp.sum(metric_row * metric_row, axis=0))
    primitive = jnp.concatenate([density[None], velocity, pressure[None]], axis=0)
    return (primitive, fluxes, speeds)


def eigen_pair(state, metric_row, pick):
    density = state[0]
    velocity = [state[1], state[2], state[3]]
    pressure = state[4]
    row_size = jnp.sqrt(metric_row[0] ** 2 + metric_row[1] ** 2 + metric_row[2] ** 2)
    normal = [metric_row[member] / row_size for member in range(3)]
    axis_unit = [1.0 if member == pick else 0.0 for member in range(3)]
    raw_cross = cross_of(normal, axis_unit)
    raw_size = jnp.sqrt(raw_cross[0] ** 2 + raw_cross[1] ** 2 + raw_cross[2] ** 2)
    tangent = [raw_cross[member] / raw_size for member in range(3)]
    binormal = cross_of(normal, tangent)
    sound_speed = jnp.sqrt(GAMMA * pressure / density)
    inverse = 1.0 / sound_speed
    kinetic = 0.5 * inner_of(velocity, velocity)
    enthalpy = GAMMA / (GAMMA - 1.0) * pressure / density + kinetic
    normal_speed = inner_of(normal, velocity)
    tangent_speed = inner_of(tangent, velocity)
    binormal_speed = inner_of(binormal, velocity)
    factor = (GAMMA - 1.0) * inverse * inverse
    scaled = factor * kinetic
    left_rows = [
        [0.5 * (scaled + normal_speed * inverse)]
        + [0.5 * (-factor * velocity[member] - normal[member] * inverse) for member in range(3)]
        + [0.5 * factor],
        [1.0 - scaled] + [factor * velocity[member] for member in range(3)] + [-factor],
        [-tangent_speed] + tangent + [0.0],
        [-binormal_speed] + binormal + [0.0],
        [0.5 * (scaled - normal_speed * inverse)]
        + [0.5 * (-factor * velocity[member] + normal[member] * inverse) for member in range(3)]
        + [0.5 * factor],
    ]
    right_columns = [
        [1.0]
        + [velocity[member] - sound_speed * normal[member] for member in range(3)]
        + [enthalpy - sound_speed * normal_speed],
        [1.0] + velocity + [kinetic],
        [0.0] + tangent + [tangent_speed],
        [0.0] + binormal + [binormal_speed],
        [1.0]
        + [velocity[member] + sound_speed * normal[member] for member in range(3)]
        + [enthalpy + sound_speed * normal_speed],
    ]
    return (left_rows, right_columns)


def project_left(matrix, vector):
    return jnp.stack(
        [
            sum((matrix[member][second] * vector[second] for second in range(5)))
            for member in range(5)
        ]
    )


def apply_right(matrix, vector):
    return jnp.stack(
        [
            sum((matrix[second][member] * vector[second] for second in range(5)))
            for member in range(5)
        ]
    )


def weno_side(stencil):
    far_left, near_left, center, near_right, far_right = stencil
    guess_zero = (2.0 * far_left - 7.0 * near_left + 11.0 * center) / 6.0
    guess_one = (-near_left + 5.0 * center + 2.0 * near_right) / 6.0
    guess_two = (2.0 * center + 5.0 * near_right - far_right) / 6.0
    smooth_zero = (
        13.0 / 12.0 * (far_left - 2.0 * near_left + center) ** 2
        + 0.25 * (far_left - 4.0 * near_left + 3.0 * center) ** 2
    )
    smooth_one = (
        13.0 / 12.0 * (near_left - 2.0 * center + near_right) ** 2
        + 0.25 * (near_left - near_right) ** 2
    )
    smooth_two = (
        13.0 / 12.0 * (center - 2.0 * near_right + far_right) ** 2
        + 0.25 * (3.0 * center - 4.0 * near_right + far_right) ** 2
    )
    weight_zero = 0.1 / (WENO_EPS + smooth_zero) ** 2
    weight_one = 0.6 / (WENO_EPS + smooth_one) ** 2
    weight_two = 0.3 / (WENO_EPS + smooth_two) ** 2
    return (weight_zero * guess_zero + weight_one * guess_one + weight_two * guess_two) / (
        weight_zero + weight_one + weight_two
    )


def interface_flux(fields, metric_row, axis, pick):
    primitive, fluxes, speeds = cell_terms(fields, metric_row)
    faces_count = fields.shape[fields.ndim + axis] - 5
    mean_state = 0.5 * (
        slab_of(primitive, 2, faces_count, axis) + slab_of(primitive, 3, faces_count, axis)
    )
    mean_row = 0.5 * (
        slab_of(metric_row, 2, faces_count, axis) + slab_of(metric_row, 3, faces_count, axis)
    )
    left_rows, right_columns = eigen_pair(mean_state, mean_row, pick)
    max_speed = slab_of(speeds, 0, faces_count, axis)
    for offset in range(1, 6):
        max_speed = jnp.maximum(max_speed, slab_of(speeds, offset, faces_count, axis))
    upwind = []
    downwind = []
    for offset in range(6):
        state_chars = project_left(left_rows, slab_of(fields, offset, faces_count, axis))
        flux_chars = project_left(left_rows, slab_of(fluxes, offset, faces_count, axis))
        upwind.append(0.5 * (flux_chars + max_speed * state_chars))
        downwind.append(0.5 * (flux_chars - max_speed * state_chars))
    combined = weno_side(upwind[0:5]) + weno_side(downwind[5:0:-1])
    return apply_right(right_columns, combined)


def divergence(fields, metric_row, axis, pick):
    face_flux = interface_flux(fields, metric_row, axis, pick)
    cells_count = face_flux.shape[face_flux.ndim + axis] - 1
    return slab_of(face_flux, 1, cells_count, axis) - slab_of(face_flux, 0, cells_count, axis)


def fix_ends(extended, at_start, at_end):
    interior = extended[..., 3:-3]
    lower_ghost = jnp.where(at_start, jnp.repeat(interior[..., :1], 3, axis=-1), extended[..., :3])
    upper_ghost = jnp.where(at_end, jnp.repeat(interior[..., -1:], 3, axis=-1), extended[..., -3:])
    return jnp.concatenate([lower_ghost, interior, upper_ghost], axis=-1)


def fix_wall(extended, ghosts, at_start, at_end):
    interior = extended[:, :, 3:-3, :]
    lower_ghost = jnp.where(at_start, ghosts, extended[:, :, :3, :])
    upper_ghost = jnp.where(
        at_end, jnp.repeat(interior[:, :, -1:, :], 3, axis=2), extended[:, :, -3:, :]
    )
    return jnp.concatenate([lower_ghost, interior, upper_ghost], axis=2)


def local(conserved, metrics, inv_volume, wake_donor):
    at_inflow = lax.axis_index("gx") == 0
    at_outflow = lax.axis_index("gx") == lax.axis_size("gx") - 1
    at_wall = lax.axis_index("gy") == 0
    at_top = lax.axis_index("gy") == lax.axis_size("gy") - 1
    mirrored = jnp.concatenate([conserved[:, :, 2::-1, :], metrics[3:6, :, 2::-1, :]], axis=0)
    count = lax.axis_size("gx")
    mirrored = lax.ppermute(mirrored, "gx", [(i, count - 1 - i) for i in range(count)])
    mirrored = mirrored[..., ::-1]
    stream = padded(jnp.concatenate([conserved, metrics[0:3]], axis=0), (("gx", 3),), 3, False)
    normal = padded(jnp.concatenate([conserved, metrics[3:6]], axis=0), (("gy", 2),), 3, False)
    span = padded(jnp.concatenate([conserved, metrics[6:9]], axis=0), (("gz", 1),), 3, True)
    stream_flow, stream_row = stream[0:5], stream[5:8]
    normal_flow, normal_row = normal[0:5], normal[5:8]
    span_flow, span_row = span[0:5], span[5:8]
    stream_flow = fix_ends(stream_flow, at_inflow, at_outflow)
    stream_row = fix_ends(stream_row, at_inflow, at_outflow)
    momentum_sign = jnp.array([1.0, -1.0, -1.0, -1.0, 1.0], dtype=jnp.float32)[:, None, None, None]
    is_wake = wake_donor >= 0
    wake_flow = jnp.where(is_wake, mirrored[0:5], conserved[:, :, 2::-1, :] * momentum_sign)
    wake_row = jnp.where(is_wake, mirrored[5:8], metrics[3:6, :, 2::-1, :])
    normal_flow = fix_wall(normal_flow, wake_flow, at_wall, at_top)
    normal_row = fix_wall(normal_row, wake_row, at_wall, at_top)
    summed = divergence(stream_flow, stream_row, -1, 1)
    summed = summed + divergence(normal_flow, normal_row, -2, 2)
    summed = summed + divergence(span_flow, span_row, -3, 0)
    time_rate = -inv_volume[None] * summed
    return (conserved + STEP_SIZE * time_rate, time_rate)


def solution(mesh):
    placed = (P(None, "gz", "gy", "gx"), P(None, "gz", "gy", "gx"), P("gz", "gy", "gx"), P("gx"))
    return jax.shard_map(
        local,
        mesh=mesh,
        in_specs=placed,
        out_specs=(P(None, "gz", "gy", "gx"), P(None, "gz", "gy", "gx")),
        check_vma=False,
    )
```
